32 devices in a mesh: seq: 8 (over z, x), exp: 4 (over y, core).
Axes of the slice: x: 2, y: 2, z: 4, core: 2. Of those that a mesh axis runs over, the one named last changes fastest.
Arguments:
- residual: bfloat16 [4096, 8192], P('seq', 'exp'), may hold values from -16 to 16
- queries: bfloat16 [4096, 4096], P('seq', 'exp'), may hold values from -6 to 6
- keys: bfloat16 [4096, 4096], P('seq', 'exp'), may hold values from -10 to 10
- values: bfloat16 [4096, 4096], P('seq', 'exp'), may hold values from -6 to 6
- documents: int32 [4096], replicated, may hold values from 0 to 1, as said below
- out_proj: bfloat16 [4096, 8192], P(None, 'exp'), may hold values from -0.09375 to 0.09375
- modality: int32 [4096], P('seq'), may hold values from 0 to 1, as said below
- norm_gain: float32 [2, 8192], P(None, 'exp'), may hold values from 0.25 to 1.75
- picks: int32 [4, 64], replicated, may hold values from 0 to 4095, as said below
- router: bfloat16 [8192, 4], P(None, 'exp'), may hold values from -0.0625 to 0.0625
- w_gate: bfloat16 [4, 8192, 4096], P('exp', None, 'seq'), may hold values from -0.0625 to 0.0625
- w_up: bfloat16 [4, 8192, 4096], P('exp', None, 'seq'), may hold values from -0.0625 to 0.0625
- w_down: bfloat16 [4, 4096, 8192], P('exp', 'seq'), may hold values from -0.09375 to 0.09375
Outputs:
- layer_out: bfloat16 [4096, 8192], P('seq', 'exp')
The draws below stay inside these ranges and needn't reach their ends.
Inputs may be any that keep to these rules, and one draw needn't show every extreme that they name: `modality`: 0 marks a text token, 1 an image token. `documents`: 0 for the first document, 1 for the second; the second begins between position 1024 and 3072. `picks`: row e lists 64 different positions in ascending order; all carry modality 0 for e < 2 and modality 1 otherwise. Within each aligned block of 512 positions (the tokens of one index of seq) a row lists at most 16 positions, and every row lists exactly 16 in some block.
All inputs are finite; a program needn't handle non-finite values.
Results may differ from the reference program's by a relative error of at most 0.0035.
Values may be sent and summed in bfloat16 or wider, within the bound.
A program may use at most 128 MiB of HBM per device.

```python
import math
import jax
import jax.numpy as jnp
from jax import lax

D = 8192
HEADS = 32
HD = 128
FF = 4096
TOK_DEV = 512
TOKENS = 4096
EXPERTS = 4
CB = 16
CAP = 64
N_SEQ = 8


def layout_draw(base_key):
    own_key = jax.random.fold_in(base_key, 11)
    span_key, force_key, pick_key = jax.random.split(own_key, 3)
    spans = 8
    span_len = TOK_DEV // spans
    span_bits = jax.random.randint(span_key, (N_SEQ, spans), 0, 2)
    one_key, two_key = jax.random.split(force_key)
    fixed_one = jax.random.randint(one_key, (N_SEQ,), 0, spans)
    offset = jax.random.randint(two_key, (N_SEQ,), 1, spans)
    second = (fixed_one + offset) % spans
    span_pos = jnp.arange(spans)
    span_bits = jnp.where(span_pos[None, :] == fixed_one[:, None], 0, span_bits)
    span_bits = jnp.where(span_pos[None, :] == second[:, None], 1, span_bits)
    modal_tags = jnp.repeat(span_bits, span_len, axis=1).astype(jnp.int32)
    flat_index = jnp.arange(TOKENS, dtype=jnp.int32)
    half_cap = CB // 2
    chosen_lists = []
    for expert in range(EXPERTS):
        modal_kind = 0 if expert < EXPERTS // 2 else 1
        order_key, shift_key, rank_key = jax.random.split(jax.random.fold_in(pick_key, expert), 3)
        shard_order = jax.random.permutation(order_key, N_SEQ)
        shift_size = jax.random.randint(shift_key, (N_SEQ // 2,), 0, half_cap + 1)
        shift_size = shift_size.at[0].set(half_cap)
        quota_rows = jnp.zeros((N_SEQ,), jnp.int32)
        quota_rows = quota_rows.at[shard_order[0::2]].set(half_cap + shift_size)
        quota_rows = quota_rows.at[shard_order[1::2]].set(half_cap - shift_size)
        shuffled = jax.vmap(lambda sub_key: jax.random.permutation(sub_key, TOK_DEV))(jax.random.split(rank_key, N_SEQ))
        sort_keys = jnp.where(modal_tags == modal_kind, shuffled, TOK_DEV + shuffled)
        rank_in = jnp.argsort(jnp.argsort(sort_keys, axis=1), axis=1)
        chosen = (rank_in < quota_rows[:, None]).reshape(TOKENS)
        listed = jnp.argsort(jnp.where(chosen, flat_index, TOKENS + flat_index))[:CAP]
        chosen_lists.append(listed.astype(jnp.int32))
    return (modal_tags.reshape(TOKENS), jnp.stack(chosen_lists))


def draw_modality(key, part):
    return layout_draw(key)[0]


def draw_picks(key, part):
    return layout_draw(key)[1]


def draw_documents(key, part):
    boundary = jax.random.randint(jax.random.fold_in(key, 5), (), TOKENS // 4, 3 * TOKENS // 4 + 1)
    return (jnp.arange(TOKENS) >= boundary).astype(jnp.int32)


def draw_queries(key, part):
    base_key = jax.random.fold_in(key, 31)
    base_draw = jnp.clip(jax.random.normal(base_key, (TOKENS, HEADS * HD), jnp.float32), -6.0, 6.0)
    return base_draw.astype(jnp.bfloat16)


def draw_keys(key, part):
    base_key = jax.random.fold_in(key, 41)
    base_draw = jnp.clip(2.5 * jax.random.normal(base_key, (TOKENS, HEADS * HD), jnp.float32), -10.0, 10.0)
    return base_draw.astype(jnp.bfloat16)


def draw_residual(key, part):
    base_key = jax.random.fold_in(jax.random.fold_in(key, 51), 0)
    rising = 0.6 + 1.2 * jnp.arange(D, dtype=jnp.float32) / D
    base_draw = jnp.clip(jax.random.normal(base_key, (TOKENS, D), jnp.float32), -4.0, 4.0)
    result = base_draw * rising[None, :]
    return jnp.clip(result, -16.0, 16.0).astype(jnp.bfloat16)


def shard_levels(key, extent, shards, smallest, top_value):
    def one(position, blocks):
        heights = jax.random.uniform(jax.random.fold_in(jax.random.fold_in(key, 6), position), (blocks,), jnp.float32, smallest / len(shards), top_value / len(shards))
        return jnp.repeat(jnp.exp(heights), extent[position] // blocks).reshape((-1,) + (1,) * (len(extent) - position - 1))

    gain = one(*shards[0])
    for cut in shards[1:]:
        gain = gain * one(*cut)
    return gain


def bell_draw(key, extent, deviation, limit, cuts=(), kind=jnp.bfloat16):
    level = shard_levels(key, extent, cuts, -0.22, 0.18) if cuts else 1.0
    entries = jax.random.normal(key, extent, jnp.float32) * deviation * level
    return jnp.minimum(jnp.maximum(entries, -limit), limit).astype(kind)


def setup_inputs(seed: int = 0) -> dict:
    arg_keys = jax.random.split(jax.random.key(seed), 14)
    return {
        "residual": draw_residual(jax.random.fold_in(arg_keys[13], 71), 0),
        "queries": draw_queries(jax.random.fold_in(arg_keys[13], 71), 0),
        "keys": draw_keys(jax.random.fold_in(arg_keys[13], 71), 0),
        "values": bell_draw(arg_keys[3], (TOKENS, HEADS * HD), 1.0, 6.0, ((0, 8), (1, 4))),
        "documents": draw_documents(jax.random.fold_in(arg_keys[13], 71), 0),
        "out_proj": bell_draw(arg_keys[5], (HEADS * HD, D), (HEADS * HD) ** -0.5, 0.09375, ((1, 4),)),
        "modality": draw_modality(jax.random.fold_in(arg_keys[13], 71), 0),
        "norm_gain": jnp.clip(1.0 + 0.15 * jax.random.normal(arg_keys[7], (2, D), jnp.float32), 0.25, 1.75),
        "picks": draw_picks(jax.random.fold_in(arg_keys[13], 71), 0),
        "router": bell_draw(arg_keys[9], (D, EXPERTS), D ** -0.5, 0.0625, ((1, 4),)),
        "w_gate": bell_draw(arg_keys[10], (EXPERTS, D, FF), D ** -0.5, 0.0625, ((0, 4), (2, 8))),
        "w_up": bell_draw(arg_keys[11], (EXPERTS, D, FF), D ** -0.5, 0.0625, ((0, 4), (2, 8))),
        "w_down": bell_draw(arg_keys[12], (EXPERTS, FF, D), FF ** -0.5, 0.09375, ((0, 4), (1, 8))),
    }


def reference(residual, queries, keys, values, documents, out_proj, modality, norm_gain, picks, router, w_gate, w_up, w_down):
    length = queries.shape[0]
    q_heads = queries.reshape(length, HEADS, HD).transpose(1, 0, 2)
    k_heads = keys.reshape(length, HEADS, HD).transpose(1, 0, 2)
    v_heads = values.reshape(length, HEADS, HD).transpose(1, 0, 2)
    positions = jnp.arange(length, dtype=jnp.int32)
    allowed = (positions[None, :] <= positions[:, None]) & (documents[None, :] == documents[:, None])

    def one_head(item):
        q_one, k_one, v_one = item
        scores = jnp.dot(q_one, k_one.T, preferred_element_type=jnp.float32) / math.sqrt(HD)
        scores = jnp.where(allowed, scores, -jnp.inf)
        row_max = lax.optimization_barrier(jnp.max(scores, axis=1))
        probs = jnp.exp(scores - row_max[:, None])
        denominator = lax.optimization_barrier(jnp.sum(probs, axis=1))
        numerator = jnp.dot(probs.astype(jnp.bfloat16), v_one, preferred_element_type=jnp.float32)
        return (numerator / denominator[:, None]).astype(jnp.bfloat16)
    attended = lax.map(one_head, (q_heads, k_heads, v_heads))
    attended = attended.transpose(1, 0, 2).reshape(length, HEADS * HD)
    hidden_state = (residual.astype(jnp.float32) + jnp.dot(attended, out_proj, preferred_element_type=jnp.float32)).astype(jnp.bfloat16)
    hidden_wide = hidden_state.astype(jnp.float32)
    mean_square = lax.optimization_barrier(jnp.mean(hidden_wide * hidden_wide, axis=1))
    gain_rows = norm_gain[modality]
    normed = (hidden_wide * lax.rsqrt(mean_square + 1e-05)[:, None] * gain_rows).astype(jnp.bfloat16)
    expert_add = jnp.zeros((length, D), jnp.float32)
    for expert in range(EXPERTS):
        chosen = normed[picks[expert]]
        gate_part = jnp.dot(chosen, w_gate[expert], preferred_element_type=jnp.float32)
        up_part = jnp.dot(chosen, w_up[expert], preferred_element_type=jnp.float32)
        inner_act = (jax.nn.silu(gate_part) * up_part).astype(jnp.bfloat16)
        summed = jnp.dot(inner_act, w_down[expert], preferred_element_type=jnp.float32)
        logits = jnp.dot(chosen, router[:, expert:expert + 1], preferred_element_type=jnp.float32)[:, 0]
        weighted = (jax.nn.sigmoid(logits)[:, None] * summed).astype(jnp.bfloat16)
        expert_add = expert_add.at[picks[expert]].add(weighted.astype(jnp.float32))
    return (hidden_wide + expert_add).astype(jnp.bfloat16)
```

```python
import functools
import math

import jax
import jax.numpy as jnp
from jax import lax
from jax.experimental import pallas as pl
from jax.experimental.pallas import tpu as pltpu
from jax.sharding import PartitionSpec as P

D = 8192
HD = 128


block_rows = 512


MESH = pl.DeviceIdType.MESH


def greet(peers):
    barrier = pltpu.get_barrier_semaphore()
    for peer in peers:
        pl.semaphore_signal(barrier, inc=1, device_id=peer, device_id_type=MESH)
    pl.semaphore_wait(barrier, len(peers))


def cut(start, size):
    return pl.ds(pl.multiple_of(start, size), size)


def heads_out_kernel(n, width, q_ref, k_ref, v_ref, qo, ko, vo, send, recv, own):
    me = lax.axis_index("seq")
    tokens = q_ref.shape[0]
    greet([{"seq": lax.rem(me + i, n)} for i in range(1, n)])
    pairs = ((k_ref, ko), (v_ref, vo), (q_ref, qo))
    copies = []
    for i in range(1, n):
        to = lax.rem(me + i, n)
        for t, (src, dst) in enumerate(pairs):
            copies.append(
                pltpu.make_async_remote_copy(
                    src_ref=src.at[:, cut(to * width, width)],
                    dst_ref=dst.at[cut(me * tokens, tokens), :],
                    send_sem=send.at[t * n + i],
                    recv_sem=recv.at[t * n + i],
                    device_id={"seq": to},
                    device_id_type=MESH,
                )
            )
            copies[-1].start()
    for t, (src, dst) in enumerate(pairs):
        copies.append(
            pltpu.make_async_copy(
                src.at[:, cut(me * width, width)], dst.at[cut(me * tokens, tokens), :], own.at[t]
            )
        )
        copies[-1].start()
    for copy in copies:
        copy.wait()


def heads_out(queries, keys, values, n):
    tokens, columns = queries.shape
    width = columns // n
    whole = jax.ShapeDtypeStruct((n * tokens, width), queries.dtype)
    anywhere = pl.BlockSpec(memory_space=pl.ANY)
    return pl.pallas_call(
        functools.partial(heads_out_kernel, n, width),
        out_shape=(whole, whole, whole),
        in_specs=[anywhere] * 3,
        out_specs=(anywhere,) * 3,
        scratch_shapes=[
            pltpu.SemaphoreType.DMA((3 * n,)),
            pltpu.SemaphoreType.DMA((3 * n,)),
            pltpu.SemaphoreType.DMA((3,)),
        ],
        compiler_params=pltpu.CompilerParams(collective_id=0, has_side_effects=True),
    )(queries, keys, values)


def heads_back_kernel(n, ny, width, a_ref, o_ref, s_send, s_recv, y_send, y_recv, c_send, c_recv, own):
    me = lax.axis_index("seq")
    place = lax.axis_index("exp")
    y, core = place // 2, lax.rem(place, 2)
    sibling = {"exp": y * 2 + 1 - core}
    across = [{"exp": lax.rem(y + k, ny) * 2 + core} for k in range(1, ny)]
    tokens = o_ref.shape[0]
    span = n * width
    greet([{"seq": lax.rem(me + i, n)} for i in range(1, n)] + across + [sibling])

    def piece(exp_at, seq_at):
        return o_ref.at[:, cut(exp_at * span + seq_at * width, width)]

    def push(src, dst, send, recv, peer):
        copy = pltpu.make_async_remote_copy(
            src_ref=src, dst_ref=dst, send_sem=send, recv_sem=recv, device_id=peer, device_id_type=MESH
        )
        copy.start()
        return copy

    local = pltpu.make_async_copy(a_ref.at[cut(me * tokens, tokens), :], piece(place, me), own)
    local.start()
    first = []
    for i in range(1, n):
        to = lax.rem(me + i, n)
        first.append(
            push(
                a_ref.at[cut(to * tokens, tokens), :],
                piece(place, me),
                s_send.at[i],
                s_recv.at[i],
                {"seq": to},
            )
        )
    second = []
    third = []
    for i in range(n):
        if i == 0:
            local.wait()
        else:
            first[i - 1].wait_recv()
        part = piece(place, lax.rem(me + n - i, n))
        for k in range(1, ny):
            at = i * ny + k
            second.append(push(part, part, y_send.at[at], y_recv.at[at], across[k - 1]))
        third.append(push(part, part, c_send.at[i * ny], c_recv.at[i * ny], sibling))
    for i in range(n):
        for k in range(1, ny):
            second[i * (ny - 1) + k - 1].wait_recv()
            at = i * ny + k
            part = piece(lax.rem(y + ny - k, ny) * 2 + core, lax.rem(me + n - i, n))
            third.append(push(part, part, c_send.at[at], c_recv.at[at], sibling))
    for copy in third:
        copy.wait_recv()
    for copy in first + second + third:
        copy.wait_send()


def heads_back(attended, n, n_exp):
    rows, width = attended.shape
    ny = n_exp // 2
    anywhere = pl.BlockSpec(memory_space=pl.ANY)
    return pl.pallas_call(
        functools.partial(heads_back_kernel, n, ny, width),
        out_shape=jax.ShapeDtypeStruct((rows // n, n_exp * n * width), attended.dtype),
        in_specs=[anywhere],
        out_specs=anywhere,
        scratch_shapes=[
            pltpu.SemaphoreType.DMA((n,)),
            pltpu.SemaphoreType.DMA((n,)),
            pltpu.SemaphoreType.DMA((n * ny,)),
            pltpu.SemaphoreType.DMA((n * ny,)),
            pltpu.SemaphoreType.DMA((n * ny,)),
            pltpu.SemaphoreType.DMA((n * ny,)),
            pltpu.SemaphoreType.DMA(()),
        ],
        compiler_params=pltpu.CompilerParams(collective_id=1, has_side_effects=True),
    )(attended)


def flash_kernel(block, border_ref, q_ref, k_ref, v_ref, o_ref):
    at = pl.program_id(1)
    border = border_ref[0]
    q_start = at * block
    rows = q_start + lax.broadcasted_iota(jnp.int32, (block, 1), 0)
    low = jnp.where(rows >= border, border, 0)
    steps = lax.broadcasted_iota(jnp.int32, (block, block), 1)
    q = q_ref[...]
    scale = math.log2(math.e) / math.sqrt(HD)

    def scored(j):
        start = pl.multiple_of(j * block, block)
        s = lax.dot_general(
            q, k_ref[pl.ds(start, block), :], (((1,), (1,)), ((), ())), preferred_element_type=jnp.float32
        )
        return s * scale, start

    def mix(p, start):
        return jnp.dot(
            p.astype(jnp.bfloat16), v_ref[pl.ds(start, block), :], preferred_element_type=jnp.float32
        )

    s, start = scored(at)
    s = jnp.where((steps >= low - start) & (steps <= rows - start), s, -jnp.inf)
    top = jnp.max(s, axis=1, keepdims=True)
    p = jnp.exp2(s - top)
    state = (top, jnp.sum(p, axis=1, keepdims=True), mix(p, start))

    def step(j, state):
        top, total, out = state
        s, start = scored(j)
        s = jnp.where(steps >= low - start, s, -jnp.inf)
        new_top = jnp.maximum(top, jnp.max(s, axis=1, keepdims=True))
        factor = jnp.exp2(top - new_top)
        p = jnp.exp2(s - new_top)
        return (
            new_top,
            total * factor + jnp.sum(p, axis=1, keepdims=True),
            out * factor + mix(p, start),
        )

    begin = jnp.where(q_start >= border, border // block, 0)
    top, total, out = lax.fori_loop(begin, at, step, state)
    o_ref[...] = (out / total).astype(o_ref.dtype)


def flash(queries, keys, values, border):
    rows, width = queries.shape
    block = block_rows
    return pl.pallas_call(
        functools.partial(flash_kernel, block),
        out_shape=jax.ShapeDtypeStruct((rows, width), queries.dtype),
        grid_spec=pltpu.PrefetchScalarGridSpec(
            num_scalar_prefetch=1,
            grid=(width // HD, rows // block),
            in_specs=[
                pl.BlockSpec((block, HD), lambda h, i, b: (i, h)),
                pl.BlockSpec((rows, HD), lambda h, i, b: (0, h)),
                pl.BlockSpec((rows, HD), lambda h, i, b: (0, h)),
            ],
            out_specs=pl.BlockSpec((block, HD), lambda h, i, b: (i, h)),
        ),
    )(border, queries, keys, values)


def attend_by_head(queries, keys, values, documents, n, n_exp):
    border = jnp.sum((documents == 0).astype(jnp.int32)).reshape(1)
    q_all, k_all, v_all = heads_out(queries, keys, values, n)
    return heads_back(flash(q_all, k_all, v_all, border), n, n_exp)


def attend_by_token(queries, keys, values, documents):
    tokens = queries.shape[0]
    heads_here = queries.shape[1] // HD
    seq_pos = lax.axis_index("seq")
    start_row = seq_pos * tokens
    query_pos = start_row + jnp.arange(tokens, dtype=jnp.int32)
    query_doc = lax.dynamic_slice_in_dim(documents, start_row, tokens, 0)
    query_heads = queries.reshape(tokens, heads_here, HD)
    score_scale = 1.0 / math.sqrt(HD)

    def attend(state, key_rows, value_rows, key_start):
        row_count = key_rows.shape[0]
        key_pos = key_start + jnp.arange(row_count, dtype=jnp.int32)
        key_doc = lax.dynamic_slice_in_dim(documents, key_start, row_count, 0)
        scores = (
            jnp.einsum(
                "qhd,khd->qhk",
                query_heads,
                key_rows.reshape(row_count, heads_here, HD),
                preferred_element_type=jnp.float32,
            )
            * score_scale
        )
        allowed = (key_pos[None, :] <= query_pos[:, None]) & (
            key_doc[None, :] == query_doc[:, None]
        )
        scores = jnp.where(allowed[:, None, :], scores, -jnp.inf)
        running_max, running_sum, running_out = state
        new_max = jnp.maximum(running_max, jnp.max(scores, axis=2))
        factor = jnp.exp(running_max - new_max)
        weights = jnp.exp(scores - new_max[:, :, None])
        running_sum = running_sum * factor + jnp.sum(weights, axis=2)
        running_out = running_out * factor[:, :, None] + jnp.einsum(
            "qhk,khd->qhd",
            weights.astype(jnp.bfloat16),
            value_rows.reshape(row_count, heads_here, HD),
            preferred_element_type=jnp.float32,
        )
        return (new_max, running_sum, running_out)

    def visit_block(state, key_rows, value_rows, key_start):
        row_count = key_rows.shape[0]
        last_doc = lax.dynamic_index_in_dim(documents, key_start + row_count - 1, 0, keepdims=False)
        beyond = (key_start > query_pos[tokens - 1]) | (last_doc < query_doc[0])
        return lax.cond(
            beyond,
            lambda inner_state: inner_state,
            lambda inner_state: attend(inner_state, key_rows, value_rows, key_start),
            state,
        )

    initial = (
        jnp.full((tokens, heads_here), -1e30, jnp.float32),
        jnp.zeros((tokens, heads_here), jnp.float32),
        jnp.zeros((tokens, heads_here, HD), jnp.float32),
    )
    state = initial
    key_piece = lax.all_gather(keys, "seq", axis=0, tiled=True)
    value_piece = lax.all_gather(values, "seq", axis=0, tiled=True)
    row_count = key_piece.shape[0]
    blocks = row_count // block_rows
    key_stack = key_piece.reshape(blocks, block_rows, key_piece.shape[1])
    value_stack = value_piece.reshape(blocks, block_rows, value_piece.shape[1])

    def scan_step(inner_state, block_item):
        block_index, key_rows, value_rows = block_item
        return (visit_block(inner_state, key_rows, value_rows, block_index * block_rows), None)

    state, unused = lax.scan(
        scan_step, state, (jnp.arange(blocks, dtype=jnp.int32), key_stack, value_stack)
    )
    running_max, running_sum, running_out = state
    attended = (
        (running_out / running_sum[:, :, None])
        .reshape(tokens, heads_here * HD)
        .astype(jnp.bfloat16)
    )
    return lax.all_gather(attended, "exp", axis=1, tiled=True)


def shards(
    residual,
    queries,
    keys,
    values,
    documents,
    out_proj,
    modality,
    norm_gain,
    picks,
    router,
    w_gate,
    w_up,
    w_down,
):
    tokens = queries.shape[0]
    seq_pos = lax.axis_index("seq")
    start_row = seq_pos * tokens
    n_seq, n_exp = lax.axis_size("seq"), lax.axis_size("exp")
    if (queries.shape[1] // HD) % n_seq == 0 and n_exp % 2 == 0:
        attended = attend_by_head(queries, keys, values, documents, n_seq, n_exp)
    else:
        attended = attend_by_token(queries, keys, values, documents)
    mixed = jnp.dot(
        attended,
        out_proj,
        preferred_element_type=jnp.float32,
    )
    hidden_state = (residual.astype(jnp.float32) + mixed).astype(jnp.bfloat16)
    hidden_wide = hidden_state.astype(jnp.float32)
    square_total = lax.psum(jnp.sum(hidden_wide * hidden_wide, axis=1), "exp")
    inverse = lax.rsqrt(square_total / D + 1e-05)
    gain_rows = jnp.where(modality[:, None] == 0, norm_gain[0][None, :], norm_gain[1][None, :])
    normed = (hidden_wide * inverse[:, None] * gain_rows).astype(jnp.bfloat16)
    capacity = tokens // 32
    inside = (picks >= start_row) & (picks < start_row + tokens)
    slot_index = jnp.cumsum(inside.astype(jnp.int32), axis=1) - 1
    matched = inside[:, None, :] & (
        slot_index[:, None, :] == jnp.arange(capacity, dtype=jnp.int32)[None, :, None]
    )
    local_index = jnp.sum(jnp.where(matched, picks[:, None, :] - start_row, 0), axis=2)
    filled = jnp.any(matched, axis=2)
    rows_out = jnp.take(normed, local_index.T, axis=0)
    rows_out = jnp.where(filled.T[:, :, None], rows_out, jnp.zeros_like(rows_out))
    arrived = lax.all_to_all(rows_out, "exp", split_axis=1, concat_axis=1, tiled=True)
    expert_rows = arrived.reshape(capacity, D)
    logits = jnp.dot(expert_rows, router, preferred_element_type=jnp.float32)[:, 0]
    piece = lax.all_gather(expert_rows, "seq", axis=0, tiled=True)
    gate_part = jnp.dot(piece, w_gate[0], preferred_element_type=jnp.float32)
    up_part = jnp.dot(piece, w_up[0], preferred_element_type=jnp.float32)
    inner_act = (jax.nn.silu(gate_part) * up_part).astype(jnp.bfloat16)
    summed = lax.psum_scatter(
        jnp.dot(inner_act, w_down[0], preferred_element_type=jnp.float32).astype(jnp.bfloat16),
        "seq",
        scatter_dimension=0,
        tiled=True,
    ).astype(jnp.float32)
    weighted = (jax.nn.sigmoid(logits)[:, None] * summed).astype(jnp.bfloat16)
    sliced = weighted.reshape(capacity, n_exp, D // n_exp)
    returned = lax.all_to_all(sliced, "exp", split_axis=1, concat_axis=0, tiled=True)
    returned = returned.reshape(n_exp * capacity, D // n_exp)
    placing = (
        (jnp.arange(tokens, dtype=jnp.int32)[:, None] == local_index.reshape(1, -1))
        & filled.reshape(1, -1)
    ).astype(jnp.bfloat16)
    expert_add = jnp.dot(placing, returned, preferred_element_type=jnp.float32)
    return (hidden_wide + expert_add).astype(jnp.bfloat16)


def solution(mesh):
    return jax.shard_map(
        shards,
        mesh=mesh,
        in_specs=(
            P("seq", "exp"),
            P("seq", "exp"),
            P("seq", "exp"),
            P("seq", "exp"),
            P(),
            P(None, "exp"),
            P("seq"),
            P(None, "exp"),
            P(),
            P(None, "exp"),
            P("exp", None, "seq"),
            P("exp", None, "seq"),
            P("exp", "seq", None),
        ),
        out_specs=P("seq", "exp"),
        check_vma=False,
    )
```

```python
import functools
import math

import jax
import jax.numpy as jnp
from jax import lax
from jax.experimental import pallas as pl
from jax.experimental.pallas import tpu as pltpu
from jax.sharding import PartitionSpec as P

D = 8192
HD = 128


block_rows = 512


MESH = pl.DeviceIdType.MESH


def greet(peers):
    barrier = pltpu.get_barrier_semaphore()
    for peer in peers:
        pl.semaphore_signal(barrier, inc=1, device_id=peer, device_id_type=MESH)
    pl.semaphore_wait(barrier, len(peers))


def cut(start, size):
    return pl.ds(pl.multiple_of(start, size), size)


def heads_out_kernel(n, width, q_ref, k_ref, v_ref, qo, ko, vo, send, recv, own):
    me = lax.axis_index("seq")
    tokens = q_ref.shape[0]
    greet([{"seq": lax.rem(me + i, n)} for i in range(1, n)])
    pairs = ((k_ref, ko), (v_ref, vo), (q_ref, qo))
    copies = []
    for i in range(1, n):
        to = lax.rem(me + i, n)
        for t, (src, dst) in enumerate(pairs):
            copies.append(
                pltpu.make_async_remote_copy(
                    src_ref=src.at[:, cut(to * width, width)],
                    dst_ref=dst.at[cut(me * tokens, tokens), :],
                    send_sem=send.at[t * n + i],
                    recv_sem=recv.at[t * n + i],
                    device_id={"seq": to},
                    device_id_type=MESH,
                )
            )
            copies[-1].start()
    for t, (src, dst) in enumerate(pairs):
        copies.append(
            pltpu.make_async_copy(
                src.at[:, cut(me * width, width)], dst.at[cut(me * tokens, tokens), :], own.at[t]
            )
        )
        copies[-1].start()
    for copy in copies:
        copy.wait()


def heads_out(queries, keys, values, n):
    tokens, columns = queries.shape
    width = columns // n
    whole = jax.ShapeDtypeStruct((n * tokens, width), queries.dtype)
    anywhere = pl.BlockSpec(memory_space=pl.ANY)
    return pl.pallas_call(
        functools.partial(heads_out_kernel, n, width),
        out_shape=(whole, whole, whole),
        in_specs=[anywhere] * 3,
        out_specs=(anywhere,) * 3,
        scratch_shapes=[
            pltpu.SemaphoreType.DMA((3 * n,)),
            pltpu.SemaphoreType.DMA((3 * n,)),
            pltpu.SemaphoreType.DMA((3,)),
        ],
        compiler_params=pltpu.CompilerParams(collective_id=0, has_side_effects=True),
    )(queries, keys, values)


def heads_back_kernel(n, ny, width, a_ref, o_ref, s_send, s_recv, y_send, y_recv, c_send, c_recv, own):
    me = lax.axis_index("seq")
    place = lax.axis_index("exp")
    y, core = place // 2, lax.rem(place, 2)
    sibling = {"exp": y * 2 + 1 - core}
    across = [{"exp": lax.rem(y + k, ny) * 2 + core} for k in range(1, ny)]
    tokens = o_ref.shape[0]
    span = n * width
    greet([{"seq": lax.rem(me + i, n)} for i in range(1, n)] + across + [sibling])

    def piece(exp_at, seq_at):
        return o_ref.at[:, cut(exp_at * span + seq_at * width, width)]

    local = pltpu.make_async_copy(a_ref.at[cut(me * tokens, tokens), :], piece(place, me), own)
    local.start()
    first = []
    for i in range(1, n):
        to = lax.rem(me + i, n)
        first.append(
            push(
                a_ref.at[cut(to * tokens, tokens), :],
                piece(place, me),
                s_send.at[i],
                s_recv.at[i],
                {"seq": to},
            )
        )
    second = []
    third = []
    for i in range(n):
        if i == 0:
            local.wait()
        else:
            first[i - 1].wait_recv()
        part = piece(place, lax.rem(me + n - i, n))
        for k in range(1, ny):
            at = i * ny + k
            second.append(push(part, part, y_send.at[at], y_recv.at[at], across[k - 1]))
        third.append(push(part, part, c_send.at[i * ny], c_recv.at[i * ny], sibling))
    for i in range(n):
        for k in range(1, ny):
            second[i * (ny - 1) + k - 1].wait_recv()
            at = i * ny + k
            part = piece(lax.rem(y + ny - k, ny) * 2 + core, lax.rem(me + n - i, n))
            third.append(push(part, part, c_send.at[at], c_recv.at[at], sibling))
    for copy in third:
        copy.wait_recv()
    for copy in first + second + third:
        copy.wait_send()


def heads_back(attended, n, n_exp):
    rows, width = attended.shape
    ny = n_exp // 2
    anywhere = pl.BlockSpec(memory_space=pl.ANY)
    return pl.pallas_call(
        functools.partial(heads_back_kernel, n, ny, width),
        out_shape=jax.ShapeDtypeStruct((rows // n, n_exp * n * width), attended.dtype),
        in_specs=[anywhere],
        out_specs=anywhere,
        scratch_shapes=[
            pltpu.SemaphoreType.DMA((n,)),
            pltpu.SemaphoreType.DMA((n,)),
            pltpu.SemaphoreType.DMA((n * ny,)),
            pltpu.SemaphoreType.DMA((n * ny,)),
            pltpu.SemaphoreType.DMA((n * ny,)),
            pltpu.SemaphoreType.DMA((n * ny,)),
            pltpu.SemaphoreType.DMA(()),
        ],
        compiler_params=pltpu.CompilerParams(collective_id=1, has_side_effects=True),
    )(attended)


def push(src, dst, send, recv, peer):
    copy = pltpu.make_async_remote_copy(
        src_ref=src, dst_ref=dst, send_sem=send, recv_sem=recv, device_id=peer, device_id_type=MESH
    )
    copy.start()
    return copy


def lines(me, nz):
    z, x = me // 2, lax.rem(me, 2)
    along = [{"seq": lax.rem(z + k, nz) * 2 + x} for k in range(1, nz)]
    return z, x, along, {"seq": z * 2 + 1 - x}


def rows_kernel(nz, ne, cap, width, r_ref, o_ref, e_send, e_recv, z_send, z_recv, x_send, x_recv, own):
    me = lax.axis_index("seq")
    place = lax.axis_index("exp")
    z, x, along, partner = lines(me, nz)
    others = [{"exp": lax.rem(place + i, ne)} for i in range(1, ne)]
    greet(others + along + [partner])

    def piece(z_at, exp_at):
        return o_ref.at[cut((z_at * 2 + x) * cap, cap), cut(exp_at * width, width)]

    local = pltpu.make_async_copy(r_ref.at[cut(place * cap, cap), :], piece(z, place), own)
    local.start()
    first = []
    for i in range(1, ne):
        src = r_ref.at[cut(lax.rem(place + i, ne) * cap, cap), :]
        first.append(push(src, piece(z, place), e_send.at[i], e_recv.at[i], others[i - 1]))
    second = []
    third = []
    for i in range(ne):
        if i == 0:
            local.wait()
        else:
            first[i - 1].wait_recv()
        part = piece(z, lax.rem(place + ne - i, ne))
        for k in range(1, nz):
            at = i * nz + k
            second.append(push(part, part, z_send.at[at], z_recv.at[at], along[k - 1]))
        third.append(push(part, part, x_send.at[i * nz], x_recv.at[i * nz], partner))
    for k in range(1, nz):
        for i in range(ne):
            second[i * (nz - 1) + k - 1].wait_recv()
            at = i * nz + k
            part = piece(lax.rem(z + nz - k, nz), lax.rem(place + ne - i, ne))
            third.append(push(part, part, x_send.at[at], x_recv.at[at], partner))
    for copy in third:
        copy.wait_recv()
    for copy in first + second + third:
        copy.wait_send()


def share_rows(rows, n, ne):
    cap, width = rows.shape[0] // ne, rows.shape[1]
    nz = n // 2
    anywhere = pl.BlockSpec(memory_space=pl.ANY)
    return pl.pallas_call(
        functools.partial(rows_kernel, nz, ne, cap, width),
        out_shape=jax.ShapeDtypeStruct((n * cap, ne * width), rows.dtype),
        in_specs=[anywhere],
        out_specs=anywhere,
        scratch_shapes=[pltpu.SemaphoreType.DMA((ne,))] * 2
        + [pltpu.SemaphoreType.DMA((ne * nz,))] * 4
        + [pltpu.SemaphoreType.DMA(())],
        compiler_params=pltpu.CompilerParams(collective_id=2, has_side_effects=True),
    )(rows)


def sums_kernel(nz, cap, p_ref, o_ref, x_buf, s_buf, z_buf, x_send, x_recv, z_send, z_recv):
    me = lax.axis_index("seq")
    z, x, along, partner = lines(me, nz)
    greet(along + [partner])

    def rows_of(k, side):
        return cut((lax.rem(z + k, nz) * 2 + side) * cap, cap)

    order = list(range(1, nz)) + [0]
    pairs = {}
    for k in order:
        pairs[k] = push(p_ref.at[rows_of(k, 1 - x), :], x_buf.at[k], x_send.at[k], x_recv.at[k], partner)
    sent = []
    for k in order:
        pairs[k].wait_recv()
        both = p_ref[rows_of(k, x), :].astype(jnp.float32) + x_buf[k].astype(jnp.float32)
        if k:
            s_buf[k] = both.astype(jnp.bfloat16)
            sent.append(push(s_buf.at[k], z_buf.at[k], z_send.at[k], z_recv.at[k], along[k - 1]))
        else:
            o_ref[...] = both
    for k in range(1, nz):
        sent[k - 1].wait_recv()
        o_ref[...] += z_buf[k].astype(jnp.float32)
    for copy in list(pairs.values()) + sent:
        copy.wait_send()


def sum_rows(partial, n):
    cap, width = partial.shape[0] // n, partial.shape[1]
    nz = n // 2
    slots = pltpu.VMEM((nz, cap, width), jnp.bfloat16)
    return pl.pallas_call(
        functools.partial(sums_kernel, nz, cap),
        out_shape=jax.ShapeDtypeStruct((cap, width), jnp.float32),
        in_specs=[pl.BlockSpec(memory_space=pltpu.VMEM)],
        out_specs=pl.BlockSpec(memory_space=pltpu.VMEM),
        scratch_shapes=[slots, slots, slots] + [pltpu.SemaphoreType.DMA((nz,))] * 4,
        compiler_params=pltpu.CompilerParams(collective_id=3, has_side_effects=True),
    )(partial)


def flash_kernel(block, border_ref, q_ref, k_ref, v_ref, o_ref):
    at = pl.program_id(1)
    border = border_ref[0]
    q_start = at * block
    rows = q_start + lax.broadcasted_iota(jnp.int32, (block, 1), 0)
    low = jnp.where(rows >= border, border, 0)
    steps = lax.broadcasted_iota(jnp.int32, (block, block), 1)
    q = q_ref[...]
    scale = math.log2(math.e) / math.sqrt(HD)

    def scored(j):
        start = pl.multiple_of(j * block, block)
        s = lax.dot_general(
            q, k_ref[pl.ds(start, block), :], (((1,), (1,)), ((), ())), preferred_element_type=jnp.float32
        )
        return s * scale, start

    def mix(p, start):
        return jnp.dot(
            p.astype(jnp.bfloat16), v_ref[pl.ds(start, block), :], preferred_element_type=jnp.float32
        )

    s, start = scored(at)
    s = jnp.where((steps >= low - start) & (steps <= rows - start), s, -jnp.inf)
    top = jnp.max(s, axis=1, keepdims=True)
    p = jnp.exp2(s - top)
    state = (top, jnp.sum(p, axis=1, keepdims=True), mix(p, start))

    def step(j, state):
        top, total, out = state
        s, start = scored(j)
        s = jnp.where(steps >= low - start, s, -jnp.inf)
        new_top = jnp.maximum(top, jnp.max(s, axis=1, keepdims=True))
        factor = jnp.exp2(top - new_top)
        p = jnp.exp2(s - new_top)
        return (
            new_top,
            total * factor + jnp.sum(p, axis=1, keepdims=True),
            out * factor + mix(p, start),
        )

    begin = jnp.where(q_start >= border, border // block, 0)
    top, total, out = lax.fori_loop(begin, at, step, state)
    o_ref[...] = (out / total).astype(o_ref.dtype)


def flash(queries, keys, values, border):
    rows, width = queries.shape
    block = block_rows
    return pl.pallas_call(
        functools.partial(flash_kernel, block),
        out_shape=jax.ShapeDtypeStruct((rows, width), queries.dtype),
        grid_spec=pltpu.PrefetchScalarGridSpec(
            num_scalar_prefetch=1,
            grid=(width // HD, rows // block),
            in_specs=[
                pl.BlockSpec((block, HD), lambda h, i, b: (i, h)),
                pl.BlockSpec((rows, HD), lambda h, i, b: (0, h)),
                pl.BlockSpec((rows, HD), lambda h, i, b: (0, h)),
            ],
            out_specs=pl.BlockSpec((block, HD), lambda h, i, b: (i, h)),
        ),
    )(border, queries, keys, values)


def attend_by_head(queries, keys, values, documents, n, n_exp):
    border = jnp.sum((documents == 0).astype(jnp.int32)).reshape(1)
    q_all, k_all, v_all = heads_out(queries, keys, values, n)
    return heads_back(flash(q_all, k_all, v_all, border), n, n_exp)


def attend_by_token(queries, keys, values, documents):
    tokens = queries.shape[0]
    heads_here = queries.shape[1] // HD
    seq_pos = lax.axis_index("seq")
    start_row = seq_pos * tokens
    query_pos = start_row + jnp.arange(tokens, dtype=jnp.int32)
    query_doc = lax.dynamic_slice_in_dim(documents, start_row, tokens, 0)
    query_heads = queries.reshape(tokens, heads_here, HD)
    score_scale = 1.0 / math.sqrt(HD)

    def attend(state, key_rows, value_rows, key_start):
        row_count = key_rows.shape[0]
        key_pos = key_start + jnp.arange(row_count, dtype=jnp.int32)
        key_doc = lax.dynamic_slice_in_dim(documents, key_start, row_count, 0)
        scores = (
            jnp.einsum(
                "qhd,khd->qhk",
                query_heads,
                key_rows.reshape(row_count, heads_here, HD),
                preferred_element_type=jnp.float32,
            )
            * score_scale
        )
        allowed = (key_pos[None, :] <= query_pos[:, None]) & (
            key_doc[None, :] == query_doc[:, None]
        )
        scores = jnp.where(allowed[:, None, :], scores, -jnp.inf)
        running_max, running_sum, running_out = state
        new_max = jnp.maximum(running_max, jnp.max(scores, axis=2))
        factor = jnp.exp(running_max - new_max)
        weights = jnp.exp(scores - new_max[:, :, None])
        running_sum = running_sum * factor + jnp.sum(weights, axis=2)
        running_out = running_out * factor[:, :, None] + jnp.einsum(
            "qhk,khd->qhd",
            weights.astype(jnp.bfloat16),
            value_rows.reshape(row_count, heads_here, HD),
            preferred_element_type=jnp.float32,
        )
        return (new_max, running_sum, running_out)

    def visit_block(state, key_rows, value_rows, key_start):
        row_count = key_rows.shape[0]
        last_doc = lax.dynamic_index_in_dim(documents, key_start + row_count - 1, 0, keepdims=False)
        beyond = (key_start > query_pos[tokens - 1]) | (last_doc < query_doc[0])
        return lax.cond(
            beyond,
            lambda inner_state: inner_state,
            lambda inner_state: attend(inner_state, key_rows, value_rows, key_start),
            state,
        )

    initial = (
        jnp.full((tokens, heads_here), -1e30, jnp.float32),
        jnp.zeros((tokens, heads_here), jnp.float32),
        jnp.zeros((tokens, heads_here, HD), jnp.float32),
    )
    state = initial
    key_piece = lax.all_gather(keys, "seq", axis=0, tiled=True)
    value_piece = lax.all_gather(values, "seq", axis=0, tiled=True)
    row_count = key_piece.shape[0]
    blocks = row_count // block_rows
    key_stack = key_piece.reshape(blocks, block_rows, key_piece.shape[1])
    value_stack = value_piece.reshape(blocks, block_rows, value_piece.shape[1])

    def scan_step(inner_state, block_item):
        block_index, key_rows, value_rows = block_item
        return (visit_block(inner_state, key_rows, value_rows, block_index * block_rows), None)

    state, unused = lax.scan(
        scan_step, state, (jnp.arange(blocks, dtype=jnp.int32), key_stack, value_stack)
    )
    running_max, running_sum, running_out = state
    attended = (
        (running_out / running_sum[:, :, None])
        .reshape(tokens, heads_here * HD)
        .astype(jnp.bfloat16)
    )
    return lax.all_gather(attended, "exp", axis=1, tiled=True)


def shards(
    residual,
    queries,
    keys,
    values,
    documents,
    out_proj,
    modality,
    norm_gain,
    picks,
    router,
    w_gate,
    w_up,
    w_down,
):
    tokens = queries.shape[0]
    seq_pos = lax.axis_index("seq")
    start_row = seq_pos * tokens
    n_seq, n_exp = lax.axis_size("seq"), lax.axis_size("exp")
    if (queries.shape[1] // HD) % n_seq == 0 and n_exp % 2 == 0:
        attended = attend_by_head(queries, keys, values, documents, n_seq, n_exp)
    else:
        attended = attend_by_token(queries, keys, values, documents)
    mixed = jnp.dot(
        attended,
        out_proj,
        preferred_element_type=jnp.float32,
    )
    hidden_state = (residual.astype(jnp.float32) + mixed).astype(jnp.bfloat16)
    hidden_wide = hidden_state.astype(jnp.float32)
    square_total = lax.psum(jnp.sum(hidden_wide * hidden_wide, axis=1), "exp")
    inverse = lax.rsqrt(square_total / D + 1e-05)
    gain_rows = jnp.where(modality[:, None] == 0, norm_gain[0][None, :], norm_gain[1][None, :])
    normed = (hidden_wide * inverse[:, None] * gain_rows).astype(jnp.bfloat16)
    capacity = tokens // 32
    inside = (picks >= start_row) & (picks < start_row + tokens)
    slot_index = jnp.cumsum(inside.astype(jnp.int32), axis=1) - 1
    matched = inside[:, None, :] & (
        slot_index[:, None, :] == jnp.arange(capacity, dtype=jnp.int32)[None, :, None]
    )
    local_index = jnp.sum(jnp.where(matched, picks[:, None, :] - start_row, 0), axis=2)
    filled = jnp.any(matched, axis=2)
    rows_out = jnp.take(normed, local_index.reshape(-1), axis=0)
    rows_out = jnp.where(filled.reshape(-1, 1), rows_out, jnp.zeros_like(rows_out))
    piece = share_rows(rows_out, n_seq, n_exp)
    expert_rows = lax.dynamic_slice_in_dim(piece, seq_pos * capacity, capacity, 0)
    logits = jnp.dot(expert_rows, router, preferred_element_type=jnp.float32)[:, 0]
    gate_part = jnp.dot(piece, w_gate[0], preferred_element_type=jnp.float32)
    up_part = jnp.dot(piece, w_up[0], preferred_element_type=jnp.float32)
    inner_act = (jax.nn.silu(gate_part) * up_part).astype(jnp.bfloat16)
    summed = sum_rows(
        jnp.dot(inner_act, w_down[0], preferred_element_type=jnp.float32).astype(jnp.bfloat16), n_seq
    )
    weighted = (jax.nn.sigmoid(logits)[:, None] * summed).astype(jnp.bfloat16)
    sliced = weighted.reshape(capacity, n_exp, D // n_exp)
    returned = lax.all_to_all(sliced, "exp", split_axis=1, concat_axis=0, tiled=True)
    returned = returned.reshape(n_exp * capacity, D // n_exp)
    placing = (
        (jnp.arange(tokens, dtype=jnp.int32)[:, None] == local_index.reshape(1, -1))
        & filled.reshape(1, -1)
    ).astype(jnp.bfloat16)
    expert_add = jnp.dot(placing, returned, preferred_element_type=jnp.float32)
    return (hidden_wide + expert_add).astype(jnp.bfloat16)


def solution(mesh):
    return jax.shard_map(
        shards,
        mesh=mesh,
        in_specs=(
            P("seq", "exp"),
            P("seq", "exp"),
            P("seq", "exp"),
            P("seq", "exp"),
            P(),
            P(None, "exp"),
            P("seq"),
            P(None, "exp"),
            P(),
            P(None, "exp"),
            P("exp", None, "seq"),
            P("exp", None, "seq"),
            P("exp", "seq", None),
        ),
        out_specs=P("seq", "exp"),
        check_vma=False,
    )
```

```python
import functools
import math

import jax
import jax.numpy as jnp
from jax import lax
from jax.experimental import pallas as pl
from jax.experimental.pallas import tpu as pltpu
from jax.sharding import PartitionSpec as P

D = 8192
HD = 128


block_rows = 512


MESH = pl.DeviceIdType.MESH


def greet(peers):
    barrier = pltpu.get_barrier_semaphore()
    for peer in peers:
        pl.semaphore_signal(barrier, inc=1, device_id=peer, device_id_type=MESH)
    pl.semaphore_wait(barrier, len(peers))


def cut(start, size):
    return pl.ds(pl.multiple_of(start, size), size)


def heads_out_kernel(n, width, q_ref, k_ref, v_ref, qo, ko, vo, send, recv, own):
    me = lax.axis_index("seq")
    tokens = q_ref.shape[0]
    greet([{"seq": lax.rem(me + i, n)} for i in range(1, n)])
    pairs = ((k_ref, ko), (v_ref, vo), (q_ref, qo))
    copies = []
    for i in range(1, n):
        to = lax.rem(me + i, n)
        for t, (src, dst) in enumerate(pairs):
            copies.append(
                pltpu.make_async_remote_copy(
                    src_ref=src.at[:, cut(to * width, width)],
                    dst_ref=dst.at[cut(me * tokens, tokens), :],
                    send_sem=send.at[t * n + i],
                    recv_sem=recv.at[t * n + i],
                    device_id={"seq": to},
                    device_id_type=MESH,
                )
            )
            copies[-1].start()
    for t, (src, dst) in enumerate(pairs):
        copies.append(
            pltpu.make_async_copy(
                src.at[:, cut(me * width, width)], dst.at[cut(me * tokens, tokens), :], own.at[t]
            )
        )
        copies[-1].start()
    for copy in copies:
        copy.wait()


def heads_out(queries, keys, values, n):
    tokens, columns = queries.shape
    width = columns // n
    whole = jax.ShapeDtypeStruct((n * tokens, width), queries.dtype)
    anywhere = pl.BlockSpec(memory_space=pl.ANY)
    return pl.pallas_call(
        functools.partial(heads_out_kernel, n, width),
        out_shape=(whole, whole, whole),
        in_specs=[anywhere] * 3,
        out_specs=(anywhere,) * 3,
        scratch_shapes=[
            pltpu.SemaphoreType.DMA((3 * n,)),
            pltpu.SemaphoreType.DMA((3 * n,)),
            pltpu.SemaphoreType.DMA((3,)),
        ],
        compiler_params=pltpu.CompilerParams(collective_id=0, has_side_effects=True),
    )(queries, keys, values)


def heads_back_kernel(n, ny, width, a_ref, o_ref, s_send, s_recv, y_send, y_recv, c_send, c_recv, own):
    me = lax.axis_index("seq")
    place = lax.axis_index("exp")
    y, core = place // 2, lax.rem(place, 2)
    sibling = {"exp": y * 2 + 1 - core}
    across = [{"exp": lax.rem(y + k, ny) * 2 + core} for k in range(1, ny)]
    tokens = o_ref.shape[0]
    span = n * width
    greet([{"seq": lax.rem(me + i, n)} for i in range(1, n)] + across + [sibling])

    def piece(exp_at, seq_at):
        return o_ref.at[:, cut(exp_at * span + seq_at * width, width)]

    local = pltpu.make_async_copy(a_ref.at[cut(me * tokens, tokens), :], piece(place, me), own)
    local.start()
    first = []
    for i in range(1, n):
        to = lax.rem(me + i, n)
        first.append(
            push(
                a_ref.at[cut(to * tokens, tokens), :],
                piece(place, me),
                s_send.at[i],
                s_recv.at[i],
                {"seq": to},
            )
        )
    second = []
    third = []
    for i in range(n):
        if i == 0:
            local.wait()
        else:
            first[i - 1].wait_recv()
        part = piece(place, lax.rem(me + n - i, n))
        for k in range(1, ny):
            at = i * ny + k
            second.append(push(part, part, y_send.at[at], y_recv.at[at], across[k - 1]))
        third.append(push(part, part, c_send.at[i * ny], c_recv.at[i * ny], sibling))
    for i in range(n):
        for k in range(1, ny):
            second[i * (ny - 1) + k - 1].wait_recv()
            at = i * ny + k
            part = piece(lax.rem(y + ny - k, ny) * 2 + core, lax.rem(me + n - i, n))
            third.append(push(part, part, c_send.at[at], c_recv.at[at], sibling))
    for copy in third:
        copy.wait_recv()
    for copy in first + second + third:
        copy.wait_send()


def heads_back(attended, n, n_exp):
    rows, width = attended.shape
    ny = n_exp // 2
    anywhere = pl.BlockSpec(memory_space=pl.ANY)
    return pl.pallas_call(
        functools.partial(heads_back_kernel, n, ny, width),
        out_shape=jax.ShapeDtypeStruct((rows // n, n_exp * n * width), attended.dtype),
        in_specs=[anywhere],
        out_specs=anywhere,
        scratch_shapes=[
            pltpu.SemaphoreType.DMA((n,)),
            pltpu.SemaphoreType.DMA((n,)),
            pltpu.SemaphoreType.DMA((n * ny,)),
            pltpu.SemaphoreType.DMA((n * ny,)),
            pltpu.SemaphoreType.DMA((n * ny,)),
            pltpu.SemaphoreType.DMA((n * ny,)),
            pltpu.SemaphoreType.DMA(()),
        ],
        compiler_params=pltpu.CompilerParams(collective_id=1, has_side_effects=True),
    )(attended)


def push(src, dst, send, recv, peer):
    copy = pltpu.make_async_remote_copy(
        src_ref=src, dst_ref=dst, send_sem=send, recv_sem=recv, device_id=peer, device_id_type=MESH
    )
    copy.start()
    return copy


def lines(me, nz):
    z, x = me // 2, lax.rem(me, 2)
    along = [{"seq": lax.rem(z + k, nz) * 2 + x} for k in range(1, nz)]
    return z, x, along, {"seq": z * 2 + 1 - x}


def ring_device(pos, n):
    half = pos // (n // 2)
    return (1 - half) * pos * 2 + half * ((n - 1 - pos) * 2 + 1)


def rows_kernel(n, ne, cap, width, r_ref, o_ref, e_send, e_recv, s_send, s_recv, own):
    me = lax.axis_index("seq")
    place = lax.axis_index("exp")
    z, x = me // 2, lax.rem(me, 2)
    pos = (1 - x) * z + x * (n - 1 - z)
    ways = (1, n - 1)
    nexts = [{"seq": ring_device(lax.rem(pos + way, n), n)} for way in ways]
    others = [{"exp": lax.rem(place + i, ne)} for i in range(1, ne)]
    greet(others + nexts)

    def piece(seq_at, exp_at):
        return o_ref.at[cut(seq_at * cap, cap), cut(exp_at * width, width)]

    local = pltpu.make_async_copy(r_ref.at[cut(place * cap, cap), :], piece(me, place), own)
    local.start()
    first = []
    for i in range(1, ne):
        src = r_ref.at[cut(lax.rem(place + i, ne) * cap, cap), :]
        first.append(push(src, piece(me, place), e_send.at[i], e_recv.at[i], others[i - 1]))
    hops = {}
    for t in range(n // 2):
        for i in range(ne):
            if t == 0:
                local.wait() if i == 0 else first[i - 1].wait_recv()
            for d in range(2):
                if t:
                    hops[i, d, t - 1].wait_recv()
                if t == n // 2 - 1 and i % 2 != d:
                    continue
                seq_at = ring_device(lax.rem(pos + n + t * (ways[1 - d]), n), n)
                part = piece(seq_at, lax.rem(place + ne - i, ne))
                at = (i * 2 + d) * (n // 2) + t
                hops[i, d, t] = push(part, part, s_send.at[at], s_recv.at[at], nexts[d])
    for i in range(ne):
        hops[i, i % 2, n // 2 - 1].wait_recv()
    for copy in first + list(hops.values()):
        copy.wait_send()


def share_rows(rows, n, ne):
    cap, width = rows.shape[0] // ne, rows.shape[1]
    anywhere = pl.BlockSpec(memory_space=pl.ANY)
    return pl.pallas_call(
        functools.partial(rows_kernel, n, ne, cap, width),
        out_shape=jax.ShapeDtypeStruct((n * cap, ne * width), rows.dtype),
        in_specs=[anywhere],
        out_specs=anywhere,
        scratch_shapes=[pltpu.SemaphoreType.DMA((ne,))] * 2
        + [pltpu.SemaphoreType.DMA((ne * n,))] * 2
        + [pltpu.SemaphoreType.DMA(())],
        compiler_params=pltpu.CompilerParams(collective_id=2, has_side_effects=True),
    )(rows)


def sums_kernel(
    nz, ne, cap, p_ref, g_ref, o_ref, x_buf, s_buf, z_buf, total, w_buf,
    x_send, x_recv, z_send, z_recv, e_send, e_recv, own,
):
    me = lax.axis_index("seq")
    z, x, along, partner = lines(me, nz)
    place = lax.axis_index("exp")
    others = [{"exp": lax.rem(place + i, ne)} for i in range(1, ne)]
    greet(along + [partner] + others)

    def rows_of(k, side):
        return cut((lax.rem(z + k, nz) * 2 + side) * cap, cap)

    order = list(range(1, nz)) + [0]
    pairs = {}
    for k in order:
        pairs[k] = push(p_ref.at[rows_of(k, 1 - x), :], x_buf.at[k], x_send.at[k], x_recv.at[k], partner)
    sent = []
    for k in order:
        pairs[k].wait_recv()
        both = p_ref[rows_of(k, x), :].astype(jnp.float32) + x_buf[k].astype(jnp.float32)
        if k:
            s_buf[k] = both.astype(jnp.bfloat16)
            sent.append(push(s_buf.at[k], z_buf.at[k], z_send.at[k], z_recv.at[k], along[k - 1]))
        else:
            total[...] = both
    for k in range(1, nz):
        sent[k - 1].wait_recv()
        total[...] += z_buf[k].astype(jnp.float32)
    w_buf[...] = (g_ref[...] * total[...]).astype(jnp.bfloat16)
    width = w_buf.shape[1] // ne
    mine = o_ref.at[cut(place * cap, cap), :]
    local = pltpu.make_async_copy(w_buf.at[:, cut(place * width, width)], mine, own)
    local.start()
    spread = []
    for i in range(1, ne):
        src = w_buf.at[:, cut(lax.rem(place + i, ne) * width, width)]
        spread.append(push(src, mine, e_send.at[i], e_recv.at[i], others[i - 1]))
    local.wait()
    for copy in spread:
        copy.wait_recv()
    for copy in list(pairs.values()) + sent + spread:
        copy.wait_send()


def sum_rows(partial, gate, n, ne):
    cap, width = partial.shape[0] // n, partial.shape[1]
    nz = n // 2
    slots = pltpu.VMEM((nz, cap, width), jnp.bfloat16)
    return pl.pallas_call(
        functools.partial(sums_kernel, nz, ne, cap),
        out_shape=jax.ShapeDtypeStruct((ne * cap, width // ne), jnp.bfloat16),
        in_specs=[pl.BlockSpec(memory_space=pltpu.VMEM)] * 2,
        out_specs=pl.BlockSpec(memory_space=pl.ANY),
        scratch_shapes=[slots, slots, slots]
        + [pltpu.VMEM((cap, width), jnp.float32), pltpu.VMEM((cap, width), jnp.bfloat16)]
        + [pltpu.SemaphoreType.DMA((nz,))] * 4
        + [pltpu.SemaphoreType.DMA((ne,))] * 2
        + [pltpu.SemaphoreType.DMA(())],
        compiler_params=pltpu.CompilerParams(collective_id=3, has_side_effects=True),
    )(partial, gate)


def flash_kernel(block, border_ref, q_ref, k_ref, v_ref, o_ref):
    at = pl.program_id(1)
    border = border_ref[0]
    q_start = at * block
    rows = q_start + lax.broadcasted_iota(jnp.int32, (block, 1), 0)
    low = jnp.where(rows >= border, border, 0)
    steps = lax.broadcasted_iota(jnp.int32, (block, block), 1)
    q = q_ref[...]
    scale = math.log2(math.e) / math.sqrt(HD)

    def scored(j):
        start = pl.multiple_of(j * block, block)
        s = lax.dot_general(
            q, k_ref[pl.ds(start, block), :], (((1,), (1,)), ((), ())), preferred_element_type=jnp.float32
        )
        return s * scale, start

    def mix(p, start):
        return jnp.dot(
            p.astype(jnp.bfloat16), v_ref[pl.ds(start, block), :], preferred_element_type=jnp.float32
        )

    s, start = scored(at)
    s = jnp.where((steps >= low - start) & (steps <= rows - start), s, -jnp.inf)
    top = jnp.max(s, axis=1, keepdims=True)
    p = jnp.exp2(s - top)
    state = (top, jnp.sum(p, axis=1, keepdims=True), mix(p, start))

    def step(j, state):
        top, total, out = state
        s, start = scored(j)
        s = jnp.where(steps >= low - start, s, -jnp.inf)
        new_top = jnp.maximum(top, jnp.max(s, axis=1, keepdims=True))
        factor = jnp.exp2(top - new_top)
        p = jnp.exp2(s - new_top)
        return (
            new_top,
            total * factor + jnp.sum(p, axis=1, keepdims=True),
            out * factor + mix(p, start),
        )

    begin = jnp.where(q_start >= border, border // block, 0)
    top, total, out = lax.fori_loop(begin, at, step, state)
    o_ref[...] = (out / total).astype(o_ref.dtype)


def flash(queries, keys, values, border):
    rows, width = queries.shape
    block = block_rows
    return pl.pallas_call(
        functools.partial(flash_kernel, block),
        out_shape=jax.ShapeDtypeStruct((rows, width), queries.dtype),
        grid_spec=pltpu.PrefetchScalarGridSpec(
            num_scalar_prefetch=1,
            grid=(width // HD, rows // block),
            in_specs=[
                pl.BlockSpec((block, HD), lambda h, i, b: (i, h)),
                pl.BlockSpec((rows, HD), lambda h, i, b: (0, h)),
                pl.BlockSpec((rows, HD), lambda h, i, b: (0, h)),
            ],
            out_specs=pl.BlockSpec((block, HD), lambda h, i, b: (i, h)),
        ),
    )(border, queries, keys, values)


def attend_by_head(queries, keys, values, documents, n, n_exp):
    border = jnp.sum((documents == 0).astype(jnp.int32)).reshape(1)
    q_all, k_all, v_all = heads_out(queries, keys, values, n)
    return heads_back(flash(q_all, k_all, v_all, border), n, n_exp)


def attend_by_token(queries, keys, values, documents):
    tokens = queries.shape[0]
    heads_here = queries.shape[1] // HD
    seq_pos = lax.axis_index("seq")
    start_row = seq_pos * tokens
    query_pos = start_row + jnp.arange(tokens, dtype=jnp.int32)
    query_doc = lax.dynamic_slice_in_dim(documents, start_row, tokens, 0)
    query_heads = queries.reshape(tokens, heads_here, HD)
    score_scale = 1.0 / math.sqrt(HD)

    def attend(state, key_rows, value_rows, key_start):
        row_count = key_rows.shape[0]
        key_pos = key_start + jnp.arange(row_count, dtype=jnp.int32)
        key_doc = lax.dynamic_slice_in_dim(documents, key_start, row_count, 0)
        scores = (
            jnp.einsum(
                "qhd,khd->qhk",
                query_heads,
                key_rows.reshape(row_count, heads_here, HD),
                preferred_element_type=jnp.float32,
            )
            * score_scale
        )
        allowed = (key_pos[None, :] <= query_pos[:, None]) & (
            key_doc[None, :] == query_doc[:, None]
        )
        scores = jnp.where(allowed[:, None, :], scores, -jnp.inf)
        running_max, running_sum, running_out = state
        new_max = jnp.maximum(running_max, jnp.max(scores, axis=2))
        factor = jnp.exp(running_max - new_max)
        weights = jnp.exp(scores - new_max[:, :, None])
        running_sum = running_sum * factor + jnp.sum(weights, axis=2)
        running_out = running_out * factor[:, :, None] + jnp.einsum(
            "qhk,khd->qhd",
            weights.astype(jnp.bfloat16),
            value_rows.reshape(row_count, heads_here, HD),
            preferred_element_type=jnp.float32,
        )
        return (new_max, running_sum, running_out)

    def visit_block(state, key_rows, value_rows, key_start):
        row_count = key_rows.shape[0]
        last_doc = lax.dynamic_index_in_dim(documents, key_start + row_count - 1, 0, keepdims=False)
        beyond = (key_start > query_pos[tokens - 1]) | (last_doc < query_doc[0])
        return lax.cond(
            beyond,
            lambda inner_state: inner_state,
            lambda inner_state: attend(inner_state, key_rows, value_rows, key_start),
            state,
        )

    initial = (
        jnp.full((tokens, heads_here), -1e30, jnp.float32),
        jnp.zeros((tokens, heads_here), jnp.float32),
        jnp.zeros((tokens, heads_here, HD), jnp.float32),
    )
    state = initial
    key_piece = lax.all_gather(keys, "seq", axis=0, tiled=True)
    value_piece = lax.all_gather(values, "seq", axis=0, tiled=True)
    row_count = key_piece.shape[0]
    blocks = row_count // block_rows
    key_stack = key_piece.reshape(blocks, block_rows, key_piece.shape[1])
    value_stack = value_piece.reshape(blocks, block_rows, value_piece.shape[1])

    def scan_step(inner_state, block_item):
        block_index, key_rows, value_rows = block_item
        return (visit_block(inner_state, key_rows, value_rows, block_index * block_rows), None)

    state, unused = lax.scan(
        scan_step, state, (jnp.arange(blocks, dtype=jnp.int32), key_stack, value_stack)
    )
    running_max, running_sum, running_out = state
    attended = (
        (running_out / running_sum[:, :, None])
        .reshape(tokens, heads_here * HD)
        .astype(jnp.bfloat16)
    )
    return lax.all_gather(attended, "exp", axis=1, tiled=True)


def shards(
    residual,
    queries,
    keys,
    values,
    documents,
    out_proj,
    modality,
    norm_gain,
    picks,
    router,
    w_gate,
    w_up,
    w_down,
):
    tokens = queries.shape[0]
    seq_pos = lax.axis_index("seq")
    start_row = seq_pos * tokens
    n_seq, n_exp = lax.axis_size("seq"), lax.axis_size("exp")
    if (queries.shape[1] // HD) % n_seq == 0 and n_exp % 2 == 0:
        attended = attend_by_head(queries, keys, values, documents, n_seq, n_exp)
    else:
        attended = attend_by_token(queries, keys, values, documents)
    mixed = jnp.dot(
        attended,
        out_proj,
        preferred_element_type=jnp.float32,
    )
    hidden_state = (residual.astype(jnp.float32) + mixed).astype(jnp.bfloat16)
    hidden_wide = hidden_state.astype(jnp.float32)
    square_total = lax.psum(jnp.sum(hidden_wide * hidden_wide, axis=1), "exp")
    inverse = lax.rsqrt(square_total / D + 1e-05)
    gain_rows = jnp.where(modality[:, None] == 0, norm_gain[0][None, :], norm_gain[1][None, :])
    normed = (hidden_wide * inverse[:, None] * gain_rows).astype(jnp.bfloat16)
    capacity = tokens // 32
    inside = (picks >= start_row) & (picks < start_row + tokens)
    slot_index = jnp.cumsum(inside.astype(jnp.int32), axis=1) - 1
    matched = inside[:, None, :] & (
        slot_index[:, None, :] == jnp.arange(capacity, dtype=jnp.int32)[None, :, None]
    )
    local_index = jnp.sum(jnp.where(matched, picks[:, None, :] - start_row, 0), axis=2)
    filled = jnp.any(matched, axis=2)
    rows_out = jnp.take(normed, local_index.reshape(-1), axis=0)
    rows_out = jnp.where(filled.reshape(-1, 1), rows_out, jnp.zeros_like(rows_out))
    piece = share_rows(rows_out, n_seq, n_exp)
    expert_rows = lax.dynamic_slice_in_dim(piece, seq_pos * capacity, capacity, 0)
    logits = jnp.dot(expert_rows, router, preferred_element_type=jnp.float32)[:, 0]
    gate_part = jnp.dot(piece, w_gate[0], preferred_element_type=jnp.float32)
    up_part = jnp.dot(piece, w_up[0], preferred_element_type=jnp.float32)
    inner_act = (jax.nn.silu(gate_part) * up_part).astype(jnp.bfloat16)
    partial = jnp.dot(inner_act, w_down[0], preferred_element_type=jnp.float32).astype(jnp.bfloat16)
    returned = sum_rows(partial, jax.nn.sigmoid(logits)[:, None], n_seq, n_exp)
    placing = (
        (jnp.arange(tokens, dtype=jnp.int32)[:, None] == local_index.reshape(1, -1))
        & filled.reshape(1, -1)
    ).astype(jnp.bfloat16)
    expert_add = jnp.dot(placing, returned, preferred_element_type=jnp.float32)
    return (hidden_wide + expert_add).astype(jnp.bfloat16)


def solution(mesh):
    return jax.shard_map(
        shards,
        mesh=mesh,
        in_specs=(
            P("seq", "exp"),
            P("seq", "exp"),
            P("seq", "exp"),
            P("seq", "exp"),
            P(),
            P(None, "exp"),
            P("seq"),
            P(None, "exp"),
            P(),
            P(None, "exp"),
            P("exp", None, "seq"),
            P("exp", None, "seq"),
            P("exp", "seq", None),
        ),
        out_specs=P("seq", "exp"),
        check_vma=False,
    )
```
